32 devices in a mesh: row: 8 (over z, core), col: 4 (over y, x).
Axes of the slice: x: 2, y: 2, z: 4, core: 2. Of those that a mesh axis runs over, the one named last changes fastest.
Arguments:
- factor: float32 [10240, 10240], P('row', 'col'), may hold values from -1 to 6, as said below
Outputs:
- progressed: float32 [10240, 10240], P('row', 'col')
The draws below stay inside these ranges and needn't reach their ends.
Inputs may be any that keep to these rules, and one draw needn't show every extreme that they name: factor is symmetric positive definite with smallest eigenvalue at least 0.5, stored in the block-cyclic order of the steps.
All inputs are finite; a program needn't handle non-finite values.
Results may differ from the reference program's by a relative error of at most 0.0001.
Values sent between devices are 32-bit elements; how exact they have to be, the bound alone decides.
A program may use at most 128 MiB of HBM per device.

```python
import jax
import jax.numpy as jnp
from jax import lax

N = 10240
TILE = 128
PIVOT = 512
STEPS = 2
N_ROW = 8
N_COL = 4


def draw_factor(key, part):
    normal_key, spread_key = jax.random.split(jax.random.fold_in(key, 11), 2)
    inner_width = 4 * PIVOT
    directions = jax.random.normal(normal_key, (N, inner_width), jnp.float32)
    weights = jnp.full((inner_width,), N / inner_width, jnp.float32)
    damping = jnp.exp(jax.random.uniform(spread_key, (N,), jnp.float32, jnp.log(0.5), jnp.log(2.0)))
    loadings = directions * jnp.sqrt(weights / N)[None, :]
    product = jnp.dot(loadings, loadings.T, precision=lax.Precision.HIGHEST, preferred_element_type=jnp.float32)
    logical = 0.5 * (product + product.T) + jnp.diag(damping)
    rows_tiles = N // (N_ROW * TILE)
    cols_tiles = N // (N_COL * TILE)
    moved = logical.reshape(rows_tiles, N_ROW, TILE, N).transpose(1, 0, 2, 3).reshape(N, N)
    moved = moved.reshape(N, cols_tiles, N_COL, TILE).transpose(0, 2, 1, 3).reshape(N, N)
    return moved.astype(jnp.float32)


def setup_inputs(seed: int = 0) -> dict:
    seeds = jax.random.split(jax.random.key(seed), 2)
    factor = draw_factor(jax.random.fold_in(seeds[1], 71), 0)
    return dict(factor=factor)


def to_logical(stored):
    rows_tiles = N // (N_ROW * TILE)
    cols_tiles = N // (N_COL * TILE)
    moved = stored.reshape(N_ROW, rows_tiles, TILE, N).transpose(1, 0, 2, 3).reshape(N, N)
    moved = moved.reshape(N, N_COL, cols_tiles, TILE).transpose(0, 2, 1, 3).reshape(N, N)
    return moved

def to_stored(logical):
    rows_tiles = N // (N_ROW * TILE)
    cols_tiles = N // (N_COL * TILE)
    moved = logical.reshape(rows_tiles, N_ROW, TILE, N).transpose(1, 0, 2, 3).reshape(N, N)
    moved = moved.reshape(N, cols_tiles, N_COL, TILE).transpose(0, 2, 1, 3).reshape(N, N)
    return moved

def reference(factor):
    matrix = to_logical(factor)
    identity = jnp.eye(PIVOT, dtype=jnp.float32)
    for step in range(STEPS):
        start = step * PIVOT
        pivot_block = matrix[start:start + PIVOT, start:start + PIVOT]
        lower = jnp.linalg.cholesky(pivot_block)
        inverse = jax.scipy.linalg.cho_solve((lower, True), identity)
        scaled = jnp.dot(inverse.astype(jnp.float32), matrix[start:start + PIVOT, :].astype(jnp.float32), precision=lax.Precision.HIGHEST, preferred_element_type=jnp.float32)
        marks = jnp.zeros((N, PIVOT), jnp.float32).at[start:start + PIVOT, :].set(identity)
        reduced = matrix[:, start:start + PIVOT] - marks
        matrix = matrix - jnp.dot(reduced.astype(jnp.float32), scaled.astype(jnp.float32), precision=lax.Precision.HIGHEST, preferred_element_type=jnp.float32)
        fixed = marks - jnp.dot(reduced.astype(jnp.float32), inverse.astype(jnp.float32), precision=lax.Precision.HIGHEST, preferred_element_type=jnp.float32)
        matrix = matrix.at[:, start:start + PIVOT].set(fixed)
    return to_stored(matrix)
```

```python
import jax
import jax.numpy as jnp
from jax import lax
from jax.experimental import pallas as pl
from jax.experimental.pallas import tpu as pltpu
from jax.sharding import PartitionSpec as P

TILE = 128
PIVOT = 512
STEPS = 2
ALL = PIVOT * STEPS
SUB = 8
HIGHEST = lax.Precision.HIGHEST


def dot32(a, b):
    return jnp.dot(a, b, precision=HIGHEST, preferred_element_type=jnp.float32)


def invert_tile(tile):
    groups = TILE // SUB
    strips = [tile[g * SUB : (g + 1) * SUB, :] for g in range(groups)]
    shape = (SUB, TILE)
    lane = lax.broadcasted_iota(jnp.int32, shape, 1)
    sub = lax.broadcasted_iota(jnp.int32, shape, 0)

    def lanes(value, column):
        return jnp.broadcast_to(value[:, column : column + 1], shape)

    def subs(value, row):
        return jnp.broadcast_to(value[row : row + 1, :], shape)

    for g in range(groups):
        first = g * SUB
        panel = strips[g]
        columns = [lanes(panel, first + m) for m in range(SUB)]
        in_group = (lane >= first) & (lane < first + SUB)
        panel = jnp.where(in_group, jnp.where(lane - first == sub, 1.0, 0.0), panel)
        for m in range(SUB):
            own = sub == m
            scale = 1.0 / subs(columns[m], m)
            factor = jnp.where(own, 0.0, columns[m])
            row = subs(panel, m) * scale
            panel = jnp.where(own, row, panel - factor * row)
            for n in range(m + 1, SUB):
                there = subs(columns[n], m) * scale
                columns[n] = jnp.where(own, there, columns[n] - factor * there)
        strips[g] = panel
        rows = [subs(panel, m) for m in range(SUB)]
        for i in range(groups):
            if i == g:
                continue
            value = strips[i]
            total = jnp.where(in_group, 0.0, value)
            for m in range(SUB):
                total = total - lanes(value, first + m) * rows[m]
            strips[i] = total
    return jnp.concatenate(strips, axis=0)


def inverse_kernel(block_ref, out_ref, row_ref, col_ref):
    size = block_ref.shape[0]
    chunk = 2 * TILE
    out_ref[...] = block_ref[...]

    def step(t, carry):
        at = pl.ds(pl.multiple_of(t * TILE, TILE), TILE)
        inverse = invert_tile(out_ref[at, at])
        row_ref[...] = dot32(inverse, out_ref[at, :])
        row_ref[:, at] = inverse
        col_ref[...] = out_ref[:, at]
        out_ref[:, at] = jnp.zeros((size, TILE), jnp.float32)
        for c in range(size // chunk):
            rows = pl.ds(c * chunk, chunk)
            out_ref[rows, :] = out_ref[rows, :] - dot32(col_ref[rows, :], row_ref[...])
        out_ref[at, :] = row_ref[...]
        return carry

    lax.fori_loop(0, size // TILE, step, 0)


def spd_inverse(block):
    size = block.shape[0]
    return pl.pallas_call(
        inverse_kernel,
        out_shape=jax.ShapeDtypeStruct((size, size), jnp.float32),
        in_specs=[pl.BlockSpec(memory_space=pltpu.VMEM)],
        out_specs=pl.BlockSpec(memory_space=pltpu.VMEM),
        scratch_shapes=[
            pltpu.VMEM((TILE, size), jnp.float32),
            pltpu.VMEM((size, TILE), jnp.float32),
        ],
        compiler_params=pltpu.CompilerParams(vmem_limit_bytes=32 << 20),
        cost_estimate=pl.CostEstimate(
            flops=60 * size**3, bytes_accessed=8 * size * size, transcendentals=0
        ),
    )(block)


def per_device(factor):
    rows_count = lax.axis_size("row")
    cols_count = lax.axis_size("col")
    local_rows, local_cols = factor.shape
    row_place = lax.axis_index("row")
    col_place = lax.axis_index("col")
    tiles = ALL // TILE
    row_slots = -(-tiles // rows_count)
    col_slots = -(-tiles // cols_count)
    row_offsets = jnp.arange(local_rows, dtype=jnp.int32)
    row_global = (row_offsets // TILE * rows_count + row_place) * TILE + row_offsets % TILE
    col_offsets = jnp.arange(local_cols, dtype=jnp.int32)
    col_global = (col_offsets // TILE * cols_count + col_place) * TILE + col_offsets % TILE
    pivots = jnp.arange(ALL, dtype=jnp.int32)

    def gather_rows(value):
        width = value.shape[1]
        got = lax.all_gather(value, "row").reshape(rows_count, row_slots, TILE, width)
        return got.transpose(1, 0, 2, 3).reshape(-1, width)[:ALL]

    def gather_cols(value):
        height = value.shape[0]
        got = lax.all_gather(value, "col").reshape(cols_count, height, col_slots, TILE)
        return got.transpose(1, 2, 0, 3).reshape(height, -1)[:, :ALL]

    row_slab = factor[: row_slots * TILE, :]
    col_slab = factor[:, : col_slots * TILE]
    pivot_block = gather_cols(gather_rows(factor[: row_slots * TILE, : col_slots * TILE]))
    pivot_block, row_slab, col_slab = lax.optimization_barrier((pivot_block, row_slab, col_slab))
    pivot_rows = gather_rows(row_slab)
    pivot_cols = gather_cols(col_slab)
    inverse = spd_inverse(pivot_block)

    row_is = row_global < ALL
    col_is = col_global < ALL
    gain = jnp.dot(
        pivot_cols, inverse, precision=lax.Precision.HIGH, preferred_element_type=jnp.float32
    )
    height = row_slots * TILE
    own = jnp.minimum(row_global[:height], ALL - 1).reshape(row_slots, TILE)[:, 0]
    own_inverse = jnp.concatenate(
        [lax.dynamic_slice(inverse, (own[s], 0), (TILE, ALL)) for s in range(row_slots)], axis=0
    )
    head = jnp.where(row_is[:height, None], -own_inverse, gain[:height])
    gain = gain.at[:height].set(head)
    width = col_slots * TILE
    marks = (pivots[:, None] == col_global[None, :width]).astype(jnp.float32)
    lead = jnp.where(col_is[None, :width], marks, pivot_rows[:, :width])
    pivot_rows = pivot_rows.at[:, :width].set(lead)
    base = jnp.where(row_is[:, None] | col_is[None, :], 0.0, factor)
    return base - jnp.dot(
        gain, pivot_rows, precision=lax.Precision.HIGH, preferred_element_type=jnp.float32
    )


def solution(mesh):
    placed = (P("row", "col"),)
    return jax.shard_map(
        per_device, mesh=mesh, in_specs=placed, out_specs=P("row", "col"), check_vma=False
    )
```

```python
import jax
import jax.numpy as jnp
from jax import lax
from jax.experimental import pallas as pl
from jax.experimental.pallas import tpu as pltpu
from jax.sharding import PartitionSpec as P

TILE = 128
PIVOT = 512
STEPS = 2
ALL = PIVOT * STEPS
SUB = 8
HIGHEST = lax.Precision.HIGHEST


def dot32(a, b):
    return jnp.dot(a, b, precision=HIGHEST, preferred_element_type=jnp.float32)


def invert_tile(tile):
    groups = TILE // SUB
    strips = [tile[g * SUB : (g + 1) * SUB, :] for g in range(groups)]
    shape = (SUB, TILE)
    lane = lax.broadcasted_iota(jnp.int32, shape, 1)
    sub = lax.broadcasted_iota(jnp.int32, shape, 0)

    def lanes(value, column):
        return jnp.broadcast_to(value[:, column : column + 1], shape)

    def subs(value, row):
        return jnp.broadcast_to(value[row : row + 1, :], shape)

    for g in range(groups):
        first = g * SUB
        panel = strips[g]
        columns = [lanes(panel, first + m) for m in range(SUB)]
        in_group = (lane >= first) & (lane < first + SUB)
        panel = jnp.where(in_group, jnp.where(lane - first == sub, 1.0, 0.0), panel)
        for m in range(SUB):
            own = sub == m
            scale = 1.0 / subs(columns[m], m)
            factor = jnp.where(own, 0.0, columns[m])
            row = subs(panel, m) * scale
            panel = jnp.where(own, row, panel - factor * row)
            for n in range(m + 1, SUB):
                there = subs(columns[n], m) * scale
                columns[n] = jnp.where(own, there, columns[n] - factor * there)
        strips[g] = panel
        rows = [subs(panel, m) for m in range(SUB)]
        for i in range(groups):
            if i == g:
                continue
            value = strips[i]
            total = jnp.where(in_group, 0.0, value)
            for m in range(SUB):
                total = total - lanes(value, first + m) * rows[m]
            strips[i] = total
    return jnp.concatenate(strips, axis=0)


def split3(value):
    high = value.astype(jnp.bfloat16)
    rest = value - high.astype(jnp.float32)
    middle = rest.astype(jnp.bfloat16)
    low = (rest - middle.astype(jnp.float32)).astype(jnp.bfloat16)
    return high, middle, low


def split2(value):
    high = value.astype(jnp.bfloat16)
    return high, (value - high.astype(jnp.float32)).astype(jnp.bfloat16)


def widen_left(value):
    high, middle, low = split3(value)
    return jnp.concatenate([high, high, middle, high, low, middle], axis=1)


def widen_right(value):
    high, middle, low = split3(value)
    return jnp.concatenate([high, middle, high, low, high, middle], axis=0)


def dot16(a, b):
    return jnp.dot(a, b, preferred_element_type=jnp.float32)


def invert_in_place(work, wide_col, wide_row):
    majors, minors, _, size = work.shape
    count = majors * minors

    def step(t, carry):
        major, minor = t // minors, t % minors
        at = pl.ds(pl.multiple_of(t * TILE, TILE), TILE)
        inverse = invert_tile(work[major, minor, :, at])
        row = dot32(inverse, work[major, minor, :, :])
        wide_col[...] = widen_left(work[:, :, :, at].reshape(count * TILE, TILE))
        work[major, minor, :, :] = row
        work[major, minor, :, at] = inverse
        row = work[major, minor, :, :]
        wide_row[...] = widen_right(row)
        work[:, :, :, at] = jnp.zeros((majors, minors, TILE, TILE), jnp.float32)
        for i in range(majors):
            left = wide_col[i * minors * TILE : (i + 1) * minors * TILE, :]
            change = dot16(left, wide_row[...]).reshape(minors, TILE, size)
            work[i] = work[i] - change
        work[major, minor, :, :] = row
        return carry

    lax.fori_loop(0, count, step, 0)


def inverse_kernel(block_ref, out_ref, wide_col, wide_row):
    out_ref[...] = block_ref[...]
    invert_in_place(out_ref, wide_col, wide_row)


def wide_scratch(size):
    return [
        pltpu.VMEM((size, 6 * TILE), jnp.bfloat16),
        pltpu.VMEM((6 * TILE, size), jnp.bfloat16),
    ]


def spd_inverse(block):
    size = block.shape[0]
    shape = (size // (2 * TILE), 2, TILE, size)
    out = pl.pallas_call(
        inverse_kernel,
        out_shape=jax.ShapeDtypeStruct(shape, jnp.float32),
        in_specs=[pl.BlockSpec(memory_space=pltpu.VMEM)],
        out_specs=pl.BlockSpec(memory_space=pltpu.VMEM),
        scratch_shapes=wide_scratch(size),
        compiler_params=pltpu.CompilerParams(vmem_limit_bytes=32 << 20),
        cost_estimate=pl.CostEstimate(
            flops=60 * size**3, bytes_accessed=8 * size * size, transcendentals=0
        ),
    )(block.reshape(shape))
    return out.reshape(size, size)


def gain_kernel(
    rows_count,
    cols_count,
    factor_ref,
    gain_high,
    gain_low,
    work,
    panel,
    wide_col,
    wide_row,
    high_ref,
    low_ref,
    local_sem,
    line_send,
    line_recv,
    plane_send,
    plane_recv,
    pair_send,
    pair_recv,
    panel_send,
    panel_recv,
):
    majors = rows_count // 2
    slots = ALL // (TILE * cols_count)
    r = lax.axis_index("row")
    c = lax.axis_index("col")
    major, minor = r // 2, r % 2
    mesh_id = pl.DeviceIdType.MESH
    pair = (major * 2 + 1 - minor, c)
    line = [(lax.rem(major + j, majors) * 2 + minor, c) for j in range(1, majors)]
    plane = [(r, lax.rem(c + j, cols_count)) for j in range(1, cols_count)]
    sources = [lax.rem(c + cols_count - j, cols_count) for j in range(cols_count)]

    barrier = pltpu.get_barrier_semaphore()
    for device in [pair] + line + plane:
        pl.semaphore_signal(barrier, inc=1, device_id=device, device_id_type=mesh_id)

    def place(slot, owner):
        return pl.ds(pl.multiple_of((slot * cols_count + owner) * TILE, TILE), TILE)

    def tile_of(slot):
        return factor_ref.at[pl.ds(0, TILE), pl.ds(slot * TILE, TILE)]

    own = []
    for s in range(slots):
        copy = pltpu.make_async_copy(
            tile_of(s), work.at[major, minor, :, place(s, c)], local_sem.at[s]
        )
        copy.start()
        own.append(copy)
    own_panel = pltpu.make_async_copy(
        factor_ref.at[:, pl.ds(0, slots * TILE)], panel.at[c], local_sem.at[slots]
    )
    own_panel.start()
    pl.semaphore_wait(barrier, 1 + len(line) + len(plane))

    line_copies = []
    for j, device in enumerate(line):
        for s in range(slots):
            copy = pltpu.make_async_remote_copy(
                src_ref=tile_of(s),
                dst_ref=work.at[major, minor, :, place(s, c)],
                send_sem=line_send.at[j, s],
                recv_sem=line_recv.at[j, s],
                device_id=device,
                device_id_type=mesh_id,
            )
            copy.start()
            line_copies.append(copy)

    def group(s, owner):
        return work.at[:, minor, :, place(s, owner)]

    def pair_group(j):
        copies = []
        for s in range(slots):
            copy = pltpu.make_async_remote_copy(
                src_ref=group(s, sources[j]),
                dst_ref=group(s, sources[j]),
                send_sem=pair_send.at[j, s],
                recv_sem=pair_recv.at[j, s],
                device_id=pair,
                device_id_type=mesh_id,
            )
            copy.start()
            copies.append(copy)
        return copies

    for copy in own:
        copy.wait()
    for copy in line_copies:
        copy.wait_recv()
    plane_copies = []
    for j, device in enumerate(plane):
        copies = []
        for s in range(slots):
            copy = pltpu.make_async_remote_copy(
                src_ref=group(s, c),
                dst_ref=group(s, c),
                send_sem=plane_send.at[j, s],
                recv_sem=plane_recv.at[j, s],
                device_id=device,
                device_id_type=mesh_id,
            )
            copy.start()
            copies.append(copy)
        plane_copies.append(copies)
    pair_copies = pair_group(0)
    for j, copies in enumerate(plane_copies):
        for copy in copies:
            copy.wait_recv()
        pair_copies += pair_group(j + 1)
    panel_copies = []
    for j, device in enumerate(plane):
        copy = pltpu.make_async_remote_copy(
            src_ref=factor_ref.at[:, pl.ds(0, slots * TILE)],
            dst_ref=panel.at[c],
            send_sem=panel_send.at[j],
            recv_sem=panel_recv.at[j],
            device_id=device,
            device_id_type=mesh_id,
        )
        copy.start()
        panel_copies.append(copy)
    for copies in plane_copies:
        for copy in copies:
            copy.wait_send()
    for copy in pair_copies:
        copy.wait()
    for copy in line_copies:
        copy.wait_send()

    invert_in_place(work, wide_col, wide_row)

    own_panel.wait()
    for copy in panel_copies:
        copy.wait()
    size = work.shape[-1]
    for i in range(majors):
        value = work[i].reshape(2 * TILE, size)
        rows = pl.ds(i * 2 * TILE, 2 * TILE)
        high_ref[rows, :], low_ref[rows, :] = split2(value)
    chunk = 2 * TILE
    half = size // 2

    @pl.loop(0, gain_high.shape[0] // chunk)
    def _(i):
        rows = pl.ds(pl.multiple_of(i * chunk, chunk), chunk)
        parts = [
            panel[owner, rows, s * TILE : (s + 1) * TILE]
            for s in range(slots)
            for owner in range(cols_count)
        ]
        left = jnp.concatenate(parts, axis=1)
        high, low = split2(left)
        for n in range(2):
            cols = slice(n * half, (n + 1) * half)
            gain = (
                dot16(high, high_ref[:, cols])
                + dot16(high, low_ref[:, cols])
                + dot16(low, high_ref[:, cols])
            )
            gain_high[rows, cols], gain_low[rows, cols] = split2(gain)

    gain_high[0:TILE, :], gain_low[0:TILE, :] = split2(-work[major, minor, :, :])


def gathered_gain(factor, rows_count, cols_count):
    height = factor.shape[0]
    majors = rows_count // 2
    slots = ALL // (TILE * cols_count)
    dma = pltpu.SemaphoreType.DMA
    return pl.pallas_call(
        lambda *refs: gain_kernel(rows_count, cols_count, *refs),
        out_shape=[jax.ShapeDtypeStruct((height, ALL), jnp.bfloat16)] * 2,
        in_specs=[pl.BlockSpec(memory_space=pl.ANY)],
        out_specs=[pl.BlockSpec(memory_space=pltpu.VMEM)] * 2,
        scratch_shapes=[
            pltpu.VMEM((majors, 2, TILE, ALL), jnp.float32),
            pltpu.VMEM((cols_count, height, slots * TILE), jnp.float32),
        ]
        + wide_scratch(ALL)
        + [
            pltpu.VMEM((ALL, ALL), jnp.bfloat16),
            pltpu.VMEM((ALL, ALL), jnp.bfloat16),
            dma((slots + 1,)),
            dma((majors - 1, slots)),
            dma((majors - 1, slots)),
            dma((cols_count - 1, slots)),
            dma((cols_count - 1, slots)),
            dma((cols_count, slots)),
            dma((cols_count, slots)),
            dma((cols_count - 1,)),
            dma((cols_count - 1,)),
        ],
        compiler_params=pltpu.CompilerParams(
            collective_id=0, has_side_effects=True, vmem_limit_bytes=40 << 20
        ),
        cost_estimate=pl.CostEstimate(
            flops=60 * ALL**3, bytes_accessed=8 * ALL * ALL, transcendentals=0
        ),
    )(factor)


def largest(extent, limit):
    return max(n for n in range(TILE, limit + 1, TILE) if extent % n == 0)


def update_kernel(
    rows_count, cols_count, gain_high, gain_low, rows_ref, base_ref, out_ref, high_ref, low_ref
):
    j, i = pl.program_id(0), pl.program_id(1)
    tall, wide = out_ref.shape
    tiles = ALL // TILE
    col_tiles = [
        (j * (wide // TILE) + n) * cols_count + lax.axis_index("col") for n in range(wide // TILE)
    ]
    row_tiles = [
        (i * (tall // TILE) + n) * rows_count + lax.axis_index("row") for n in range(tall // TILE)
    ]

    @pl.when(i == 0)
    def _():
        high_ref[...], low_ref[...] = split2(rows_ref[...])

        for n, tile in enumerate(col_tiles):

            @pl.when(tile < tiles)
            def _(n=n, tile=tile):
                cols = slice(n * TILE, (n + 1) * TILE)
                down = lax.broadcasted_iota(jnp.int32, (ALL, TILE), 0)
                across = lax.broadcasted_iota(jnp.int32, (ALL, TILE), 1)
                marks = jnp.where(down - across == tile * TILE, 1.0, 0.0)
                high_ref[:, cols] = marks.astype(jnp.bfloat16)
                low_ref[:, cols] = jnp.zeros((ALL, TILE), jnp.bfloat16)

    rows = pl.ds(pl.multiple_of(i * tall, tall), tall)
    high, low = gain_high[rows, :], gain_low[rows, :]
    change = (
        dot16(high, high_ref[...]) + dot16(high, low_ref[...]) + dot16(low, high_ref[...])
    )
    out_ref[...] = base_ref[...] - change

    for m, row_tile in enumerate(row_tiles):
        for n, col_tile in enumerate(col_tiles):

            @pl.when((row_tile < tiles) | (col_tile < tiles))
            def _(m=m, n=n):
                part = (slice(m * TILE, (m + 1) * TILE), slice(n * TILE, (n + 1) * TILE))
                out_ref[part] = -change[part]


def update(gain_high, gain_low, pivot_rows, factor, rows_count, cols_count):
    height, width = factor.shape
    tall, wide = largest(height, 2 * TILE), largest(width, 5 * TILE)
    whole = pl.BlockSpec(gain_high.shape, lambda j, i: (0, 0), pipeline_mode=pl.Buffered(1))
    block = pl.BlockSpec((tall, wide), lambda j, i: (i, j))
    return pl.pallas_call(
        lambda *refs: update_kernel(rows_count, cols_count, *refs),
        out_shape=jax.ShapeDtypeStruct(factor.shape, jnp.float32),
        grid=(width // wide, height // tall),
        in_specs=[whole, whole, pl.BlockSpec((ALL, wide), lambda j, i: (0, j)), block],
        out_specs=block,
        scratch_shapes=[pltpu.VMEM((ALL, wide), jnp.bfloat16)] * 2,
        compiler_params=pltpu.CompilerParams(vmem_limit_bytes=40 << 20),
        cost_estimate=pl.CostEstimate(
            flops=6 * height * width * ALL, bytes_accessed=12 * height * width, transcendentals=0
        ),
    )(gain_high, gain_low, pivot_rows, factor)


def per_device(factor):
    rows_count = lax.axis_size("row")
    cols_count = lax.axis_size("col")
    row_place = lax.axis_index("row")
    tiles = ALL // TILE
    row_slots = -(-tiles // rows_count)
    col_slots = -(-tiles // cols_count)
    def gather_rows(value):
        width = value.shape[1]
        got = lax.all_gather(value, "row").reshape(rows_count, row_slots, TILE, width)
        return got.transpose(1, 0, 2, 3).reshape(-1, width)[:ALL]

    def gather_cols(value):
        height = value.shape[0]
        got = lax.all_gather(value, "col").reshape(cols_count, height, col_slots, TILE)
        return got.transpose(1, 2, 0, 3).reshape(height, -1)[:, :ALL]

    if rows_count == tiles and cols_count > 1 and tiles % cols_count == 0:
        pivot_rows = gather_rows(factor[:TILE, :])
        gain_high, gain_low = gathered_gain(factor, rows_count, cols_count)
    else:
        row_slab = factor[: row_slots * TILE, :]
        col_slab = factor[:, : col_slots * TILE]
        pivot_block = gather_cols(gather_rows(factor[: row_slots * TILE, : col_slots * TILE]))
        pivot_block, row_slab, col_slab = lax.optimization_barrier(
            (pivot_block, row_slab, col_slab)
        )
        pivot_rows = gather_rows(row_slab)
        pivot_cols = gather_cols(col_slab)
        inverse = spd_inverse(pivot_block)
        gain = jnp.dot(
            pivot_cols, inverse, precision=lax.Precision.HIGH, preferred_element_type=jnp.float32
        )
        for s in range(row_slots):
            own = s * rows_count + row_place
            start = jnp.minimum(own, tiles - 1) * TILE
            head = gain[s * TILE : (s + 1) * TILE]
            head = jnp.where(own < tiles, -lax.dynamic_slice(inverse, (start, 0), head.shape), head)
            gain = gain.at[s * TILE : (s + 1) * TILE].set(head)
        gain_high = lax.reduce_precision(gain, 8, 7)
        gain_low = (gain - gain_high).astype(jnp.bfloat16)
        gain_high = gain_high.astype(jnp.bfloat16)
    return update(gain_high, gain_low, pivot_rows, factor, rows_count, cols_count)


def solution(mesh):
    placed = (P("row", "col"),)
    return jax.shard_map(
        per_device, mesh=mesh, in_specs=placed, out_specs=P("row", "col"), check_vma=False
    )
```

```python
import jax
import jax.numpy as jnp
from jax import lax
from jax.experimental import pallas as pl
from jax.experimental.pallas import tpu as pltpu
from jax.sharding import PartitionSpec as P

TILE = 128
PIVOT = 512
STEPS = 2
ALL = PIVOT * STEPS
SUB = 8
HIGHEST = lax.Precision.HIGHEST


def dot32(a, b):
    return jnp.dot(a, b, precision=HIGHEST, preferred_element_type=jnp.float32)


def invert_tile(tile):
    groups = TILE // SUB
    strips = [tile[g * SUB : (g + 1) * SUB, :] for g in range(groups)]
    shape = (SUB, TILE)
    lane = lax.broadcasted_iota(jnp.int32, shape, 1)
    sub = lax.broadcasted_iota(jnp.int32, shape, 0)

    def lanes(value, column):
        return jnp.broadcast_to(value[:, column : column + 1], shape)

    def subs(value, row):
        return jnp.broadcast_to(value[row : row + 1, :], shape)

    for g in range(groups):
        first = g * SUB
        panel = strips[g]
        columns = [lanes(panel, first + m) for m in range(SUB)]
        in_group = (lane >= first) & (lane < first + SUB)
        panel = jnp.where(in_group, jnp.where(lane - first == sub, 1.0, 0.0), panel)
        for m in range(SUB):
            own = sub == m
            scale = 1.0 / subs(columns[m], m)
            factor = jnp.where(own, 0.0, columns[m])
            row = subs(panel, m) * scale
            panel = jnp.where(own, row, panel - factor * row)
            for n in range(m + 1, SUB):
                there = subs(columns[n], m) * scale
                columns[n] = jnp.where(own, there, columns[n] - factor * there)
        strips[g] = panel
        rows = [subs(panel, m) for m in range(SUB)]
        for i in range(groups):
            if i == g:
                continue
            value = strips[i]
            total = jnp.where(in_group, 0.0, value)
            for m in range(SUB):
                total = total - lanes(value, first + m) * rows[m]
            strips[i] = total
    return jnp.concatenate(strips, axis=0)


def split3(value):
    high = value.astype(jnp.bfloat16)
    rest = value - high.astype(jnp.float32)
    middle = rest.astype(jnp.bfloat16)
    low = (rest - middle.astype(jnp.float32)).astype(jnp.bfloat16)
    return high, middle, low


def split2(value):
    high = value.astype(jnp.bfloat16)
    return high, (value - high.astype(jnp.float32)).astype(jnp.bfloat16)


def widen_left(value):
    high, middle, low = split3(value)
    return jnp.concatenate([high, high, middle, high, low, middle], axis=1)


def widen_right(value):
    high, middle, low = split3(value)
    return jnp.concatenate([high, middle, high, low, high, middle], axis=0)


def dot16(a, b):
    return jnp.dot(a, b, preferred_element_type=jnp.float32)


def invert_in_place(work, wide_col, wide_row, first, last):
    majors, minors, _, size = work.shape
    count = majors * minors

    def step(t, carry):
        major, minor = t // minors, t % minors
        at = pl.ds(pl.multiple_of(t * TILE, TILE), TILE)
        inverse = invert_tile(work[major, minor, :, at])
        row = dot32(inverse, work[major, minor, :, :])
        wide_col[...] = widen_left(work[:, :, :, at].reshape(count * TILE, TILE))
        work[major, minor, :, :] = row
        work[major, minor, :, at] = inverse
        row = work[major, minor, :, :]
        wide_row[...] = widen_right(row)
        work[:, :, :, at] = jnp.zeros((majors, minors, TILE, TILE), jnp.float32)
        for i in range(majors):
            left = wide_col[i * minors * TILE : (i + 1) * minors * TILE, :]
            change = dot16(left, wide_row[...]).reshape(minors, TILE, size)
            work[i] = work[i] - change
        work[major, minor, :, :] = row
        return carry

    lax.fori_loop(first, last, step, 0)


def inverse_kernel(block_ref, out_ref, wide_col, wide_row):
    out_ref[...] = block_ref[...]
    invert_in_place(out_ref, wide_col, wide_row, 0, out_ref.shape[0] * out_ref.shape[1])


def wide_scratch(size):
    return [
        pltpu.VMEM((size, 6 * TILE), jnp.bfloat16),
        pltpu.VMEM((6 * TILE, size), jnp.bfloat16),
    ]


def spd_inverse(block):
    size = block.shape[0]
    shape = (size // (2 * TILE), 2, TILE, size)
    out = pl.pallas_call(
        inverse_kernel,
        out_shape=jax.ShapeDtypeStruct(shape, jnp.float32),
        in_specs=[pl.BlockSpec(memory_space=pltpu.VMEM)],
        out_specs=pl.BlockSpec(memory_space=pltpu.VMEM),
        scratch_shapes=wide_scratch(size),
        compiler_params=pltpu.CompilerParams(vmem_limit_bytes=32 << 20),
        cost_estimate=pl.CostEstimate(
            flops=60 * size**3, bytes_accessed=8 * size * size, transcendentals=0
        ),
    )(block.reshape(shape))
    return out.reshape(size, size)


def gain_kernel(
    rows_count,
    cols_count,
    factor_ref,
    gain_high,
    gain_low,
    work,
    panel,
    wide_col,
    wide_row,
    high_ref,
    low_ref,
    local_sem,
    line_send,
    line_recv,
    plane_send,
    plane_recv,
    pair_send,
    pair_recv,
    panel_send,
    panel_recv,
    ready,
):
    majors = rows_count // 2
    slots = ALL // (TILE * cols_count)
    r = lax.axis_index("row")
    c = lax.axis_index("col")
    major, minor = r // 2, r % 2
    mesh_id = pl.DeviceIdType.MESH
    pair = (major * 2 + 1 - minor, c)
    line = [(lax.rem(major + j, majors) * 2 + minor, c) for j in range(1, majors)]
    plane = [(r, lax.rem(c + j, cols_count)) for j in range(1, cols_count)]
    sources = [lax.rem(c + cols_count - j, cols_count) for j in range(cols_count)]

    barrier = pltpu.get_barrier_semaphore()
    for device in [pair] + line + plane:
        pl.semaphore_signal(barrier, inc=1, device_id=device, device_id_type=mesh_id)

    def place(slot, owner):
        return pl.ds(pl.multiple_of((slot * cols_count + owner) * TILE, TILE), TILE)

    def tile_of(slot):
        return factor_ref.at[pl.ds(0, TILE), pl.ds(slot * TILE, TILE)]

    own = []
    for s in range(slots):
        copy = pltpu.make_async_copy(
            tile_of(s), work.at[major, minor, :, place(s, c)], local_sem.at[s]
        )
        copy.start()
        own.append(copy)
    own_panel = pltpu.make_async_copy(
        factor_ref.at[:, pl.ds(0, slots * TILE)], panel.at[c], local_sem.at[slots]
    )
    own_panel.start()
    pl.semaphore_wait(barrier, 1 + len(line) + len(plane))

    line_copies = []
    for j, device in enumerate(line):
        copies = []
        for s in range(slots):
            copy = pltpu.make_async_remote_copy(
                src_ref=tile_of(s),
                dst_ref=work.at[major, minor, :, place(s, c)],
                send_sem=line_send.at[j, s],
                recv_sem=line_recv.at[j, s],
                device_id=device,
                device_id_type=mesh_id,
            )
            copy.start()
            copies.append(copy)
        line_copies.append(copies)

    plane_copies = [[] for _ in plane]
    for j in range(majors):
        source = lax.rem(major + majors - j, majors)
        for copy in line_copies[j - 1] if j else own:
            if j:
                copy.wait_recv()
            else:
                copy.wait()
        for p, device in enumerate(plane):
            for s in range(slots):
                copy = pltpu.make_async_remote_copy(
                    src_ref=work.at[source, minor, :, place(s, c)],
                    dst_ref=work.at[source, minor, :, place(s, c)],
                    send_sem=plane_send.at[j, p, s],
                    recv_sem=plane_recv.at[j, p, s],
                    device_id=device,
                    device_id_type=mesh_id,
                )
                copy.start()
                plane_copies[p].append(copy)

    def pair_group(j):
        copies = []
        for s in range(slots):
            group = work.at[:, minor, :, place(s, sources[j])]
            copy = pltpu.make_async_remote_copy(
                src_ref=group,
                dst_ref=group,
                send_sem=pair_send.at[j, s],
                recv_sem=pair_recv.at[j, s],
                device_id=pair,
                device_id_type=mesh_id,
            )
            copy.start()
            copies.append(copy)
        return copies

    pair_copies = pair_group(0)
    for p, copies in enumerate(plane_copies):
        for copy in copies:
            copy.wait_recv()
        pair_copies += pair_group(p + 1)
    for device in plane:
        pl.semaphore_signal(ready, inc=1, device_id=device, device_id_type=mesh_id)
    for copies in plane_copies + line_copies:
        for copy in copies:
            copy.wait_send()
    for copy in pair_copies:
        copy.wait()

    invert_in_place(work, wide_col, wide_row, 0, 1)

    pl.semaphore_wait(ready, len(plane))
    panel_copies = []
    for j, device in enumerate(plane):
        copy = pltpu.make_async_remote_copy(
            src_ref=factor_ref.at[:, pl.ds(0, slots * TILE)],
            dst_ref=panel.at[c],
            send_sem=panel_send.at[j],
            recv_sem=panel_recv.at[j],
            device_id=device,
            device_id_type=mesh_id,
        )
        copy.start()
        panel_copies.append(copy)

    invert_in_place(work, wide_col, wide_row, 1, majors * 2)

    own_panel.wait()
    for copy in panel_copies:
        copy.wait()
    size = work.shape[-1]
    for i in range(majors):
        value = work[i].reshape(2 * TILE, size)
        rows = pl.ds(i * 2 * TILE, 2 * TILE)
        high_ref[rows, :], low_ref[rows, :] = split2(value)
    chunk = 2 * TILE
    half = size // 2

    @pl.loop(0, gain_high.shape[0] // chunk)
    def _(i):
        rows = pl.ds(pl.multiple_of(i * chunk, chunk), chunk)
        parts = [
            panel[owner, rows, s * TILE : (s + 1) * TILE]
            for s in range(slots)
            for owner in range(cols_count)
        ]
        left = jnp.concatenate(parts, axis=1)
        high, low = split2(left)
        for n in range(2):
            cols = slice(n * half, (n + 1) * half)
            gain = (
                dot16(high, high_ref[:, cols])
                + dot16(high, low_ref[:, cols])
                + dot16(low, high_ref[:, cols])
            )
            gain_high[rows, cols], gain_low[rows, cols] = split2(gain)

    gain_high[0:TILE, :], gain_low[0:TILE, :] = split2(-work[major, minor, :, :])


def gathered_gain(factor, rows_count, cols_count):
    height = factor.shape[0]
    majors = rows_count // 2
    slots = ALL // (TILE * cols_count)
    dma = pltpu.SemaphoreType.DMA
    return pl.pallas_call(
        lambda *refs: gain_kernel(rows_count, cols_count, *refs),
        out_shape=[jax.ShapeDtypeStruct((height, ALL), jnp.bfloat16)] * 2,
        in_specs=[pl.BlockSpec(memory_space=pl.ANY)],
        out_specs=[pl.BlockSpec(memory_space=pltpu.VMEM)] * 2,
        scratch_shapes=[
            pltpu.VMEM((majors, 2, TILE, ALL), jnp.float32),
            pltpu.VMEM((cols_count, height, slots * TILE), jnp.float32),
        ]
        + wide_scratch(ALL)
        + [
            pltpu.VMEM((ALL, ALL), jnp.bfloat16),
            pltpu.VMEM((ALL, ALL), jnp.bfloat16),
            dma((slots + 1,)),
            dma((majors - 1, slots)),
            dma((majors - 1, slots)),
            dma((majors, cols_count - 1, slots)),
            dma((majors, cols_count - 1, slots)),
            dma((cols_count, slots)),
            dma((cols_count, slots)),
            dma((cols_count - 1,)),
            dma((cols_count - 1,)),
            pltpu.SemaphoreType.REGULAR,
        ],
        compiler_params=pltpu.CompilerParams(
            collective_id=0, has_side_effects=True, vmem_limit_bytes=40 << 20
        ),
        cost_estimate=pl.CostEstimate(
            flops=60 * ALL**3, bytes_accessed=8 * ALL * ALL, transcendentals=0
        ),
    )(factor)


def largest(extent, limit):
    return max(n for n in range(TILE, limit + 1, TILE) if extent % n == 0)


def update_kernel(
    rows_count, cols_count, gain_high, gain_low, rows_ref, base_ref, out_ref, wide_ref
):
    j, i = pl.program_id(0), pl.program_id(1)
    tall, wide = out_ref.shape
    tiles = ALL // TILE
    col_tiles = [
        (j * (wide // TILE) + n) * cols_count + lax.axis_index("col") for n in range(wide // TILE)
    ]
    row_tiles = [
        (i * (tall // TILE) + n) * rows_count + lax.axis_index("row") for n in range(tall // TILE)
    ]

    @pl.when(i == 0)
    def _():
        high, low = split2(rows_ref[...])
        wide_ref[0:ALL, :] = high
        wide_ref[ALL : 2 * ALL, :] = low
        wide_ref[2 * ALL : 3 * ALL, :] = high

        for n, tile in enumerate(col_tiles):

            @pl.when(tile < tiles)
            def _(n=n, tile=tile):
                cols = slice(n * TILE, (n + 1) * TILE)
                down = lax.broadcasted_iota(jnp.int32, (ALL, TILE), 0)
                across = lax.broadcasted_iota(jnp.int32, (ALL, TILE), 1)
                marks = jnp.where(down - across == tile * TILE, 1.0, 0.0).astype(jnp.bfloat16)
                wide_ref[0:ALL, cols] = marks
                wide_ref[ALL : 2 * ALL, cols] = jnp.zeros((ALL, TILE), jnp.bfloat16)
                wide_ref[2 * ALL : 3 * ALL, cols] = marks

    rows = pl.ds(pl.multiple_of(i * tall, tall), tall)
    high, low = gain_high[rows, :], gain_low[rows, :]
    change = dot16(jnp.concatenate([high, high, low], axis=1), wide_ref[...])
    out_ref[...] = base_ref[...] - change

    for m, row_tile in enumerate(row_tiles):
        for n, col_tile in enumerate(col_tiles):

            @pl.when((row_tile < tiles) | (col_tile < tiles))
            def _(m=m, n=n):
                part = (slice(m * TILE, (m + 1) * TILE), slice(n * TILE, (n + 1) * TILE))
                out_ref[part] = -change[part]


def update(gain_high, gain_low, pivot_rows, factor, rows_count, cols_count):
    height, width = factor.shape
    tall, wide = largest(height, 5 * TILE), largest(width, 5 * TILE)
    whole = pl.BlockSpec(gain_high.shape, lambda j, i: (0, 0), pipeline_mode=pl.Buffered(1))
    block = pl.BlockSpec((tall, wide), lambda j, i: (i, j))
    return pl.pallas_call(
        lambda *refs: update_kernel(rows_count, cols_count, *refs),
        out_shape=jax.ShapeDtypeStruct(factor.shape, jnp.float32),
        grid=(width // wide, height // tall),
        in_specs=[whole, whole, pl.BlockSpec((ALL, wide), lambda j, i: (0, j)), block],
        out_specs=block,
        scratch_shapes=[pltpu.VMEM((3 * ALL, wide), jnp.bfloat16)],
        compiler_params=pltpu.CompilerParams(vmem_limit_bytes=40 << 20),
        cost_estimate=pl.CostEstimate(
            flops=6 * height * width * ALL, bytes_accessed=12 * height * width, transcendentals=0
        ),
    )(gain_high, gain_low, pivot_rows, factor)


def per_device(factor):
    rows_count = lax.axis_size("row")
    cols_count = lax.axis_size("col")
    row_place = lax.axis_index("row")
    tiles = ALL // TILE
    row_slots = -(-tiles // rows_count)
    col_slots = -(-tiles // cols_count)
    def gather_rows(value):
        width = value.shape[1]
        got = lax.all_gather(value, "row").reshape(rows_count, row_slots, TILE, width)
        return got.transpose(1, 0, 2, 3).reshape(-1, width)[:ALL]

    def gather_cols(value):
        height = value.shape[0]
        got = lax.all_gather(value, "col").reshape(cols_count, height, col_slots, TILE)
        return got.transpose(1, 2, 0, 3).reshape(height, -1)[:, :ALL]

    if rows_count == tiles and cols_count > 1 and tiles % cols_count == 0:
        pivot_rows = gather_rows(factor[:TILE, :])
        gain_high, gain_low = gathered_gain(factor, rows_count, cols_count)
    else:
        row_slab = factor[: row_slots * TILE, :]
        col_slab = factor[:, : col_slots * TILE]
        pivot_block = gather_cols(gather_rows(factor[: row_slots * TILE, : col_slots * TILE]))
        pivot_block, row_slab, col_slab = lax.optimization_barrier(
            (pivot_block, row_slab, col_slab)
        )
        pivot_rows = gather_rows(row_slab)
        pivot_cols = gather_cols(col_slab)
        inverse = spd_inverse(pivot_block)
        gain = jnp.dot(
            pivot_cols, inverse, precision=lax.Precision.HIGH, preferred_element_type=jnp.float32
        )
        for s in range(row_slots):
            own = s * rows_count + row_place
            start = jnp.minimum(own, tiles - 1) * TILE
            head = gain[s * TILE : (s + 1) * TILE]
            head = jnp.where(own < tiles, -lax.dynamic_slice(inverse, (start, 0), head.shape), head)
            gain = gain.at[s * TILE : (s + 1) * TILE].set(head)
        gain_high = lax.reduce_precision(gain, 8, 7)
        gain_low = (gain - gain_high).astype(jnp.bfloat16)
        gain_high = gain_high.astype(jnp.bfloat16)
    return update(gain_high, gain_low, pivot_rows, factor, rows_count, cols_count)


def solution(mesh):
    placed = (P("row", "col"),)
    return jax.shard_map(
        per_device, mesh=mesh, in_specs=placed, out_specs=P("row", "col"), check_vma=False
    )
```
